32 devices in a mesh: groups: 2 (over x), ind: 16 (over z, y, core).
Axes of the slice: x: 2, y: 2, z: 4, core: 2. Of those that a mesh axis runs over, the one named last changes fastest.
Arguments:
- genotype: bfloat16 [12288, 16384], P(('groups', 'ind')), parts along dimension 0, may hold values from -4 to 4
- residual: bfloat16 [12288, 256], P(('groups', 'ind')), parts along dimension 0, may hold values from -4 to 4
- labels: int32 [12288, 256], P(('groups', 'ind')), parts along dimension 0, may hold values 0 or 1
- incl_old: float32 [32768, 256], P(('groups', 'ind')), parts along dimension 0, may hold values from 0.02 to 0.98
- mean_old: float32 [32768, 256], P(('groups', 'ind')), parts along dimension 0, may hold values from -0.078125 to 0.078125
- prior_logit: float32 [256], replicated, may hold values from -4 to 0
- slab_scale: float32 [256], replicated, may hold values from 0.25 to 8
- offset: float32 [256], replicated, may hold values from -2 to 1
Outputs:
- incl_new: float32 [32768, 256], P(('groups', 'ind')), parts along dimension 0
- mean_new: float32 [32768, 256], P(('groups', 'ind')), parts along dimension 0
- resid_new: float32 [12288, 256], P(('groups', 'ind')), parts along dimension 0
The draws below stay inside these ranges and needn't reach their ends.
There are 2 independent parts, one for each index of `groups`. The reference program is written for one: setup_inputs(seed, part) draws one part's arguments, and reference() takes and returns one part's arrays. A program takes and returns all parts, laid end to end along the dimension named above; an argument that names none is the same for every part. Nothing has to cross between parts.
All inputs are finite; a program needn't handle non-finite values. No bound on the sum of `labels` on one device may be relied on, other than what follows from the above.
Results may differ from the reference program's by a relative error of at most 0.00062.
Values may be sent and summed in bfloat16 or wider, within the bound.
A program may use at most 128 MiB of HBM per device.

```python
import math
import jax
import jax.numpy as jnp

NVAR = 16384
COLS = 256
NIND = 6144


def with_ends(entries, own_key, least, top_value):
    shape = entries.shape
    index_at = [jax.random.randint(jax.random.fold_in(own_key, axis), (), 0, shape[axis]) for axis in range(len(shape))]
    entries = entries.at[tuple(index_at)].set(least)
    longest = shape.index(max(shape))
    index_at[longest] = (index_at[longest] + 1) % shape[longest]
    return entries.at[tuple(index_at)].set(top_value)


def spiked(result, own_key, source, target, blocks, factor):
    def block_of(axis_at):
        return (jnp.arange(result.shape[axis_at]) // (result.shape[axis_at] // blocks)).reshape((-1,) + (1,) * (result.ndim - 1 - axis_at))

    one_side = jax.random.permutation(own_key, blocks)[block_of(target)]
    other_side = (block_of(target) + blocks // 2) % blocks
    return jnp.where((block_of(source) == one_side) | (block_of(source) == other_side), factor * result, result)


def shard_levels(key, dims, cuts, low, largest):
    level, own = 1.0, jax.random.fold_in(key, 6)
    for axis_at, shards_of in cuts:
        draws = jnp.exp(jax.random.uniform(jax.random.fold_in(own, axis_at), (shards_of,), jnp.float32, low / len(cuts), largest / len(cuts)))
        level = level * jnp.repeat(draws, dims[axis_at] // shards_of).reshape([-1 if axis == axis_at else 1 for axis in range(len(dims))])
    return level


def centred(own_key, shape, spread, bound, split=(), held_as=jnp.bfloat16):
    values = spread * jax.random.normal(own_key, shape, jnp.float32)
    if split:
        values = values * shard_levels(own_key, shape, split, -0.22, 0.18)
    return jnp.clip(values, -bound, bound).astype(held_as)


def heavy_noise(key, shape, scale, reach, cuts, heavy, dtype=jnp.bfloat16):
    drawn = scale * jax.random.normal(key, shape, jnp.float32)
    if cuts:
        drawn = drawn * shard_levels(key, shape, cuts, -0.22, 0.18)
    return jnp.clip(spiked(drawn, jax.random.fold_in(key, 3), *heavy), -reach, reach).astype(dtype)


def setup_inputs(seed: int = 0, part: int = 0) -> dict:
    arg_keys = jax.random.split(jax.random.key(seed), 9)
    part_splits = jax.random.split(jax.random.fold_in(arg_keys[8], part), 9)
    genotype = heavy_noise(part_splits[0], (NIND, NVAR), 1.0, 4.0, ((0, 16),), (0, 1, 16, 2.0))
    residual = centred(part_splits[1], (NIND, COLS), 1.5, 4.0, ((0, 16),))
    labels = with_ends((jax.random.randint(part_splits[2], (NIND, COLS), 0, 2) < 1).astype(jnp.int32), jax.random.fold_in(part_splits[2], 1), 0, 1)
    incl_old = jnp.clip(0.02 + 0.96000002 * jax.random.uniform(part_splits[3], (NVAR, COLS), jnp.float32) ** shard_levels(part_splits[3], (NVAR, COLS), ((0, 16),), -0.2, 0.2), 0.02, 0.98)
    mean_old = centred(part_splits[4], (NVAR, COLS), NIND ** -0.5, 0.078125, ((0, 16),), jnp.float32)
    prior_logit = jnp.clip(jax.random.uniform(arg_keys[5], (COLS,), jnp.float32, -4.0, 0.0), -4.0, 0.0)
    slab_scale = jnp.clip(jnp.exp(jax.random.uniform(arg_keys[6], (COLS,), jnp.float32, math.log(0.25), math.log(8.0))), 0.25, 8.0)
    offset = jnp.clip(jax.random.uniform(arg_keys[7], (COLS,), jnp.float32, -2.0, 1.0), -2.0, 1.0)
    return dict(genotype=genotype, residual=residual, labels=labels, incl_old=incl_old, mean_old=mean_old, prior_logit=prior_logit, slab_scale=slab_scale, offset=offset)


def reference(genotype, residual, labels, incl_old, mean_old, prior_logit, slab_scale, offset):
    corr = jnp.dot(genotype.T, residual, preferred_element_type=jnp.float32)
    stat = corr / NIND + incl_old * mean_old
    shrink = slab_scale / (1.0 + slab_scale)
    mean_new = stat * shrink
    logit = prior_logit - 0.5 * jnp.log1p(slab_scale) + 0.5 * NIND * shrink * stat * stat
    incl_new = 0.5 * incl_old + 0.5 * jax.nn.sigmoid(logit)
    effect = (incl_new * mean_new).astype(jnp.bfloat16)
    eta = jnp.dot(genotype, effect, preferred_element_type=jnp.float32) + offset
    resid_new = 4.0 * (labels.astype(jnp.float32) - jax.nn.sigmoid(eta))
    return incl_new, mean_new, resid_new
```

```python
import functools
import math

import jax
import jax.numpy as jnp
from jax import lax
from jax.experimental import pallas as pl
from jax.experimental.pallas import tpu as pltpu
from jax.sharding import PartitionSpec as P

LARGEST_TERM = 64.0

REDUCE_WIDE = (0, 5,)
GATHER_WIDE = (2,)
PLAN = {
    "P0": 12.910, "P1": 15.610, "P2": 15.620, "P3": 16.930, "P4": 17.370, "T0Y": 17.380, "T0Z": 17.380,
    "T1Z": 18.250, "T1Y": 18.310, "T2Y": 18.970, "T2Z": 19.380, "ARY": 19.770, "FIY": 19.780,
    "ARZ": 20.700, "FIZ": 21.680, "g1Z": 21.690, "OT": 21.690, "g1Y": 22.060, "g2Z": 22.700,
    "g3Z": 22.710, "h1Z": 22.750, "g2Y": 22.910, "h2Z": 23.400, "g3Y": 23.710, "LA": 25.800,
    "h3Z": 26.710, "U1": 26.720, "U2": 26.730,
}


def plan(length):
    if length == 4:
        return PLAN
    steps = {"P0": -3.0, "P1": -2.9, "P2": -2.8, "P3": -2.7, "P4": -2.6}
    for k in "YZ":
        for t in range(length - 1):
            steps[f"T{t}{k}"] = t + 0.9 - 0.02 * t
        steps["AR" + k] = length + 0.5
        steps["FI" + k] = length + 1.4
        for u in range(1, length):
            steps[f"g{u}{k}"] = length + 1 + u + 0.35 - 0.02 * u
            steps[f"h{u}Z"] = length + 2 + u + 0.34 - 0.02 * u
    steps["OT"] = length + 2.36
    steps["LA"] = 2 * length + 2.9
    steps["U1"] = 2 * length + 3.92
    steps["U2"] = 2 * length + 4.95
    return steps


def sweep_kernel(
    n, chunks, slots,
    geno_hbm, resid_ref, incl_hbm, mean_hbm, prior_ref, scale_ref,
    stat_out, eta,
    geno, incl, mean, core_out, core_in, pair_out, pair_in, own, line_out, line_in, eff,
    geno_sem, in_sem, core_ss, core_rs, pair_ss, pair_rs, line_ss, line_rs,
    gz_ss, gz_rs, gy_ss, gy_rs, gc_ss, gc_rs,
):
    length = n // 4
    owned = incl.shape[0]
    rows = owned // chunks
    people = resid_ref.shape[0]
    total = float(people * n)
    coding = 32760.0 / math.log(1.0 + LARGEST_TERM * total)
    me = lax.axis_index("ind")
    z = me // 4
    y = (me // 2) % 2
    c = me % 2

    def at(zz, yy, cc):
        return zz * 4 + yy * 2 + cc

    core_dev = {"ind": at(z, y, 1 - c)}
    pair_dev = {"ind": at(z, 1 - y, c)}
    up_dev = {"ind": at(lax.rem(z + 1, length), y, c)}
    down_dev = {"ind": at(lax.rem(z + length - 1, length), y, c)}
    has_up = z < length - 1
    has_down = z > 0

    def remote(src, dst, ss, rs, dev):
        return pltpu.make_async_remote_copy(
            src_ref=src, dst_ref=dst, send_sem=ss, recv_sem=rs,
            device_id=dev, device_id_type=pl.DeviceIdType.MESH,
        )

    def encode(x):
        code = (jnp.log(1.0 + jnp.abs(x)) * coding + 0.5).astype(jnp.int32)
        return jnp.where(x < 0.0, -code, code).astype(jnp.int16)

    def decode(code):
        level = code.astype(jnp.int32).astype(jnp.float32)
        size = jnp.exp(jnp.abs(level) * (1.0 / coding)) - 1.0
        return jnp.where(level < 0.0, -size, size)

    def loop(count, body):
        lax.fori_loop(0, count, lambda i, _: (body(i), 0)[1], 0)

    def for_z(body):
        loop(length, body)

    def place_of(zz, yy, cc):
        return (cc * 2 + yy) * length + zz

    def span(first, count=1):
        return pl.ds(pl.multiple_of(first * rows, math.gcd(rows, 128)), count * rows)

    def load(s, zz, yy, cc):
        q = place_of(zz, yy, cc)
        return pltpu.make_async_copy(
            geno_hbm.at[:, pl.ds(pl.multiple_of(at(zz, yy, cc) * owned + s * rows, 128), rows)],
            geno.at[s, :, span(q)], geno_sem.at[s, q],
        )

    owners = ((1 - y, 1 - c), (1 - y, c), (y, 1 - c), (y, c))

    def load_chunk(s):
        for yy, cc in owners:
            for_z(lambda i: load(s, i, yy, cc).start())

    loop(chunks, load_chunk)
    small = [
        pltpu.make_async_copy(incl_hbm, incl, in_sem.at[0]),
        pltpu.make_async_copy(mean_hbm, mean, in_sem.at[1]),
    ]
    for copy in small:
        copy.start()

    barrier = pltpu.get_barrier_semaphore()
    pl.semaphore_signal(barrier, inc=1, device_id=core_dev, device_id_type=pl.DeviceIdType.MESH)
    pl.semaphore_signal(barrier, inc=1, device_id=pair_dev, device_id_type=pl.DeviceIdType.MESH)

    @pl.when(has_up)
    def _():
        pl.semaphore_signal(barrier, inc=1, device_id=up_dev, device_id_type=pl.DeviceIdType.MESH)

    @pl.when(has_down)
    def _():
        pl.semaphore_signal(barrier, inc=1, device_id=down_dev, device_id_type=pl.DeviceIdType.MESH)

    pl.semaphore_wait(barrier, 2 + has_up.astype(jnp.int32) + has_down.astype(jnp.int32))

    for copy in small:
        copy.wait()
    eta[...] = jnp.zeros_like(eta)
    scale = scale_ref[...]
    shrink = scale / (1.0 + scale)
    bias = prior_ref[...] - 0.5 * jnp.log1p(scale)
    curve = 0.5 * total * shrink

    def among(s, which):
        found = s < 0
        for k in which:
            found = found | (s == k)
        return found

    def reduce_wide(s):
        return among(s, REDUCE_WIDE)

    def gather_wide(s):
        return among(s, GATHER_WIDE)

    def product(s, yy, cc, out):
        for_z(lambda i: load(s, i, yy, cc).wait())

        def piece(j):
            out[span(4 * j, 4), :] = lax.dot_general(
                geno[s, :, span(place_of(4 * j, yy, cc), 4)], resid_ref[...], (((0,), (0,)), ((), ())),
                preferred_element_type=jnp.float32,
            )

        loop(length // 4, piece)

    def core_copy(s, h):
        k = lax.rem(s, slots)
        return remote(
            core_out.at[k, h], core_in.at[s, h], core_ss.at[s, h], core_rs.at[s, h], core_dev
        )

    def pair_copy(s):
        return remote(pair_out.at[s], pair_in.at[s], pair_ss.at[s], pair_rs.at[s], pair_dev)

    def pair_last(s):
        return remote(
            pair_out.at[s, span(0)], pair_in.at[s, span(0)], pair_ss.at[s], pair_rs.at[s], pair_dev
        )

    def line_copy(s, t, d, g):
        return remote(
            line_out.at[s, t, d, g], line_in.at[s, t, d, g], line_ss.at[s, t, d, g], line_rs.at[s, t, d, g],
            up_dev if d == 0 else down_dev,
        )

    def to_core(s, h, yy):
        @pl.when(s >= slots)
        def _():
            core_copy(s - slots, h).wait_send()

        product(s, yy, 1 - c, core_out.at[lax.rem(s, slots), h])
        core_copy(s, h).start()

    def first_core(s):
        to_core(s, 0, 1 - y)

    def first_own(s):
        product(s, 1 - y, c, own.at[s, 1])

    def first_pair(s):
        core_copy(s, 0).wait_recv()

        @pl.when(jnp.logical_not(reduce_wide(s)))
        def _():
            def piece(j):
                part = span(4 * j, 4)
                pair_out[s, part] = encode(own[s, 1, part] + core_in[s, 0, part])

            loop(length // 4, piece)
            pair_copy(s).start()

        @pl.when(reduce_wide(s))
        def _():
            def piece(j):
                part = span(4 * j, 4)
                own[s, 1, part] = own[s, 1, part] + core_in[s, 0, part]

            loop(length // 4, piece)

    def second_core(s):
        to_core(s, 1, y)
        product(s, y, c, own.at[s, 0])

    def second_own(s):
        core_copy(s, 1).wait_recv()

        def piece(j):
            part = span(4 * j, 4)
            own[s, 0, part] = own[s, 0, part] + core_in[s, 1, part]

        loop(length // 4, piece)

    def along(s, t, wide):
        if t == 0 and not wide:
            pair_copy(s).wait_recv()

            def piece(j):
                part = span(4 * j, 4)
                own[s, 0, part] = own[s, 0, part] + decode(pair_in[s, part])

            loop(length // 4, piece)

        for d in range(2):
            place = z if d == 0 else length - 1 - z
            block = length - 1 - t + z if d == 0 else t - (length - 1 - z)

            for g in range(2 if wide else 1):
                @pl.when((place == 0) & (place < length - 1))
                def _():
                    line_out[s, t, d, g] = encode(own[s, g, span(block)])
                    line_copy(s, t, d, g).start()

                if t > 0:
                    @pl.when((place > 0) & (place <= t) & (place < length - 1))
                    def _():
                        line_copy(s, t - 1, d, g).wait_recv()
                        line_out[s, t, d, g] = encode(own[s, g, span(block)] + decode(line_in[s, t - 1, d, g]))
                        line_copy(s, t, d, g).start()

    def arrive(s, wide):
        for g in range(2 if wide else 1):
            for d in range(2):
                @pl.when(has_down if d == 0 else has_up)
                def _():
                    line_copy(s, length - 2, d, g).wait_recv()
                    own[s, g, span(z)] = own[s, g, span(z)] + decode(line_in[s, length - 2, d, g])

        if wide:
            pair_out[s, span(0)] = encode(own[s, 1, span(z)])
            pair_last(s).start()

    def gz_copy(s, u, d, f):
        k, q = 2 * s + f, span(place_of(z - u if d == 0 else z + u, y if f == 0 else 1 - y, c))
        return remote(
            eff.at[s, q], eff.at[s, q], gz_ss.at[k, u, d], gz_rs.at[k, u, d], up_dev if d == 0 else down_dev
        )

    def gz_landed(s, u, d, f):
        k, q = 2 * s + f, span(place_of(z - 1 - u if d == 0 else z + 1 + u, y if f == 0 else 1 - y, c))
        return remote(
            eff.at[s, q], eff.at[s, q], gz_ss.at[k, u, d], gz_rs.at[k, u, d], up_dev if d == 0 else down_dev
        )

    def gy_copy(s, i, yy):
        q = span(place_of(i, yy, c))
        return remote(eff.at[s, q], eff.at[s, q], gy_ss.at[s, i], gy_rs.at[s, i], pair_dev)

    def gc_copy(s, i, yy, cc):
        q = span(place_of(i, yy, cc))
        return remote(eff.at[s, q], eff.at[s, q], gc_ss.at[s, yy, i], gc_rs.at[s, yy, i], core_dev)

    def use(s, cc):
        def piece(j):
            q = span(place_of(0, 0, cc) + 8 * j, 8)
            eta[...] += jnp.dot(geno[s, :, q], eff[s, q], preferred_element_type=jnp.float32)

        loop(length // 4, piece)

    def send_own(s, f):
        @pl.when(has_up)
        def _():
            gz_copy(s, 0, 0, f).start()

        @pl.when(has_down)
        def _():
            gz_copy(s, 0, 1, f).start()

        gc_copy(s, z, y if f == 0 else 1 - y, c).start()

    def finish(s, wide):
        if wide:
            pair_last(s).wait_recv()
            own[s, 0, span(z)] = own[s, 0, span(z)] + decode(pair_in[s, span(0)])
        here = pl.ds(pl.multiple_of(s * rows, 8), rows)
        before = incl[here, :]
        stat = own[s, 0, span(z)] / total + before * mean[here, :]
        stat_out[here, :] = stat
        incl_new = 0.5 * before + 0.5 * jax.nn.sigmoid(bias + curve * stat * stat)
        eff[s, span(place_of(z, y, c))] = (incl_new * (stat * shrink)).astype(jnp.bfloat16)
        gy_copy(s, z, y).start()
        send_own(s, 0)

    def send_other(s):
        gy_copy(s, z, 1 - y).wait_recv()
        send_own(s, 1)

    def spread(s, u, f, wide):
        for d in range(2):
            source = z - u if d == 0 else z + u

            @pl.when((source >= 0) & (source < length))
            def _():
                gz_landed(s, u - 1, d, f).wait_recv()

                if u < length - 1:
                    @pl.when(has_up if d == 0 else has_down)
                    def _():
                        gz_copy(s, u, d, f).start()

                if not wide:
                    gy_copy(s, source, y).start()

                gc_copy(s, source, y if f == 0 else 1 - y, c).start()

    def from_pair(s):
        def take(i):
            gy_copy(s, i, 1 - y).wait_recv()
            gc_copy(s, i, 1 - y, c).start()

        for_z(take)

    def use_own(s):
        use(s, c)

    def use_core(s):
        def take(i):
            for yy in range(2):
                gc_copy(s, i, yy, 1 - c).wait_recv()

        for_z(take)
        use(s, 1 - c)

    tasks = {
        "P0": (None, None, first_core), "P1": (None, None, first_own), "P2": (None, None, first_pair),
        "P3": (None, None, second_core), "P4": (None, None, second_own),
        "OT": (gather_wide, True, send_other), "LA": (gather_wide, False, from_pair),
        "U1": (None, None, use_own), "U2": (None, None, use_core),
    }
    for kind in "YZ":
        wide = kind == "Z"
        for t in range(length - 1):
            tasks[f"T{t}{kind}"] = (reduce_wide, wide, functools.partial(along, t=t, wide=wide))
        tasks["AR" + kind] = (reduce_wide, wide, functools.partial(arrive, wide=wide))
        tasks["FI" + kind] = (reduce_wide, wide, functools.partial(finish, wide=wide))
        for u in range(1, length):
            tasks[f"g{u}{kind}"] = (gather_wide, wide, functools.partial(spread, u=u, f=0, wide=wide))
            if wide:
                tasks[f"h{u}Z"] = (gather_wide, True, functools.partial(spread, u=u, f=1, wide=True))

    steps = plan(length)
    least = min(math.floor(steps[name]) for name in tasks)
    late = {name: math.floor(steps[name]) - least for name in tasks}
    order = sorted(tasks, key=lambda name: steps[name] - math.floor(steps[name]))

    def wave(w):
        for name in order:
            test, wanted, body = tasks[name]
            s = w - late[name]
            go = (s >= 0) & (s < chunks)
            if test is not None:
                go = go & (test(s) if wanted else jnp.logical_not(test(s)))

            @pl.when(go)
            def _():
                body(s)

    loop(chunks + max(late.values()), wave)

    def drain(s):
        @pl.when(s >= chunks - slots)
        def _():
            for h in range(2):
                core_copy(s, h).wait_send()

        @pl.when(reduce_wide(s))
        def _():
            pair_last(s).wait_send()

        @pl.when(jnp.logical_not(reduce_wide(s)))
        def _():
            pair_copy(s).wait_send()

        gy_copy(s, z, y).wait_send()

        @pl.when(jnp.logical_not(gather_wide(s)))
        def _():
            def sent(i):
                @pl.when(i != z)
                def _():
                    gy_copy(s, i, y).wait_send()

            for_z(sent)

        def step(t):
            for d in range(2):
                place = z if d == 0 else length - 1 - z
                origin = z - t if d == 0 else z + t

                @pl.when((place <= t) & (place < length - 1))
                def _():
                    line_copy(s, t, d, 0).wait_send()

                    @pl.when(reduce_wide(s))
                    def _():
                        line_copy(s, t, d, 1).wait_send()

                @pl.when((origin >= 0) & (origin < length) & (place < length - 1))
                def _():
                    gz_copy(s, t, d, 0).wait_send()

                    @pl.when(gather_wide(s))
                    def _():
                        gz_copy(s, t, d, 1).wait_send()

        loop(length - 1, step)

        def blocks(i):
            for yy in range(2):
                gc_copy(s, i, yy, c).wait_send()

        for_z(blocks)

    loop(chunks, drain)


def outputs_kernel(
    half_total, stat_ref, incl_ref, eta_ref, labels_ref, prior_ref, scale_ref, offset_ref,
    incl_out, mean_out, resid_out,
):
    scale = scale_ref[...]
    shrink = scale / (1.0 + scale)
    bias = prior_ref[...] - 0.5 * jnp.log1p(scale)
    stat = stat_ref[...]
    mean_out[...] = stat * shrink
    logit = bias + (half_total * shrink) * stat * stat
    incl_out[...] = 0.5 * incl_ref[...] + 0.5 * jax.nn.sigmoid(logit)
    resid_out[...] = 4.0 * (
        labels_ref[...].astype(jnp.float32) - jax.nn.sigmoid(eta_ref[...] + offset_ref[...])
    )


def on_device(genotype, residual, labels, incl_old, mean_old, prior_logit, slab_scale, offset):
    n = lax.axis_size("ind")
    people, _ = genotype.shape
    owned, columns = incl_old.shape
    length = n // 4
    chunks = max(1, min(8, owned // 128))
    slots = max(1, min(chunks // 2, 3))
    rows = owned // chunks
    f32, bf16, i16 = jnp.float32, jnp.bfloat16, jnp.int16
    anywhere = pl.BlockSpec(memory_space=pl.ANY)
    vmem = pl.BlockSpec(memory_space=pltpu.VMEM)
    dma = pltpu.SemaphoreType.DMA
    hops = length - 1
    prior, scale, shift = (v.reshape(1, -1) for v in (prior_logit, slab_scale, offset))
    stat, eta = pl.pallas_call(
        functools.partial(sweep_kernel, n, chunks, slots),
        out_shape=(
            jax.ShapeDtypeStruct((owned, columns), f32),
            jax.ShapeDtypeStruct((people, columns), f32),
        ),
        in_specs=[anywhere, vmem, anywhere, anywhere, vmem, vmem],
        out_specs=(vmem, vmem),
        scratch_shapes=[
            pltpu.VMEM((chunks, people, n * rows), bf16),
            pltpu.VMEM(incl_old.shape, f32),
            pltpu.VMEM(mean_old.shape, f32),
            pltpu.VMEM((slots, 2, length * rows, columns), f32),
            pltpu.VMEM((chunks, 2, length * rows, columns), f32),
            pltpu.VMEM((chunks, length * rows, columns), i16),
            pltpu.VMEM((chunks, length * rows, columns), i16),
            pltpu.VMEM((chunks, 2, length * rows, columns), f32),
            pltpu.VMEM((chunks, hops, 2, 2, rows, columns), i16),
            pltpu.VMEM((chunks, hops, 2, 2, rows, columns), i16),
            pltpu.VMEM((chunks, n * rows, columns), bf16),
            dma((chunks, n)),
            dma((2,)),
            dma((chunks, 2)),
            dma((chunks, 2)),
            dma((chunks,)),
            dma((chunks,)),
            dma((chunks, hops, 2, 2)),
            dma((chunks, hops, 2, 2)),
            dma((2 * chunks, hops, 2)),
            dma((2 * chunks, hops, 2)),
            dma((chunks, length)),
            dma((chunks, length)),
            dma((chunks, 2, length)),
            dma((chunks, 2, length)),
        ],
        compiler_params=pltpu.CompilerParams(
            collective_id=0, has_side_effects=True, vmem_limit_bytes=67043328
        ),
        name="sweep",
    )(genotype, residual, incl_old, mean_old, prior, scale)

    steps = 4 if owned % 32 == 0 and people % 32 == 0 else 1
    upper = pl.BlockSpec((owned // steps, columns), lambda i: (i, 0))
    lower = pl.BlockSpec((people // steps, columns), lambda i: (i, 0))
    flat = pl.BlockSpec((1, columns), lambda i: (0, 0))
    return pl.pallas_call(
        functools.partial(outputs_kernel, 0.5 * people * n),
        grid=(steps,),
        out_shape=(
            jax.ShapeDtypeStruct((owned, columns), f32),
            jax.ShapeDtypeStruct((owned, columns), f32),
            jax.ShapeDtypeStruct((people, columns), f32),
        ),
        in_specs=[upper, upper, lower, lower, flat, flat, flat],
        out_specs=(upper, upper, lower),
        name="outputs",
    )(stat, incl_old, eta, labels, prior, scale, shift)


def solution(mesh):
    placed = (
        P(("groups", "ind"), None),
        P(("groups", "ind"), None),
        P(("groups", "ind"), None),
        P(("groups", "ind"), None),
        P(("groups", "ind"), None),
        P(),
        P(),
        P(),
    )
    return jax.shard_map(
        on_device,
        mesh=mesh,
        in_specs=placed,
        out_specs=(
            P(("groups", "ind"), None),
            P(("groups", "ind"), None),
            P(("groups", "ind"), None),
        ),
        check_vma=False,
    )
```

```python
import functools
import math

import jax
import jax.numpy as jnp
from jax import lax
from jax.experimental import pallas as pl
from jax.experimental.pallas import tpu as pltpu
from jax.sharding import PartitionSpec as P

LARGEST_TERM = 64.0

REDUCE_WIDE = (2, 6,)
GATHER_WIDE = (5,)
PLAN = {
    "P0": -10.032, "P1": -9.486, "P3": -9.133, "P2": -8.792, "P4": -8.681, "E0Z": -8.235, "E1Z": -7.941,
    "T1Z": -7.542, "D0Y": -7.169, "E0Y": -7.165, "E2Z": -6.876, "T2Z": -6.771, "D1Y": -6.701,
    "E1Y": -6.697, "T1Y": -6.070, "D2Y": -6.002, "ARZ": -5.824, "D3Y": -5.508, "E2Y": -5.073,
    "T2Y": -4.946, "ARY": -3.931, "FIZ": -3.901, "FIY": -3.855, "g1Y": -2.207, "g1Z": -2.031,
    "g2Y": -1.049, "OT": -0.847, "g3Y": -0.345, "h1Z": 1.041, "g2Z": 1.986, "g3Z": 3.677, "LA": 4.014,
    "h2Z": 4.121, "h3Z": 4.228, "U1": 4.766, "U2": 5.410,
}


def plan(length):
    if length == 4:
        return PLAN
    steps = {"P0": -3.0, "P1": -2.9, "P2": -2.8, "P3": -2.7, "P4": -2.6}
    for t in range(length):
        steps[f"D{t}Y"] = 0.5 + 0.01 * t
    for k in "YZ":
        for t in range(length - 1):
            steps[f"E{t}{k}"] = steps[f"T{t}{k}"] = t + 0.9 - 0.02 * t
        steps["AR" + k] = length + 0.5
        steps["FI" + k] = length + 1.4
        for u in range(1, length):
            steps[f"g{u}{k}"] = length + 1 + u + 0.35 - 0.02 * u
            steps[f"h{u}Z"] = length + 2 + u + 0.34 - 0.02 * u
    steps["OT"] = length + 2.36
    steps["LA"] = 2 * length + 2.9
    steps["U1"] = 2 * length + 4.92
    steps["U2"] = 2 * length + 5.95
    return steps


def sweep_kernel(
    n, chunks, per, slots,
    geno_hbm, resid_ref, incl_hbm, mean_hbm, prior_ref, scale_ref,
    stat_out, eta,
    geno, incl, mean, core_out, core_in, pair_out, pair_in, own, line_out, line_in, eff,
    geno_sem, in_sem, core_ss, core_rs, pair_ss, pair_rs, line_ss, line_rs,
    gz_ss, gz_rs, gy_ss, gy_rs, gc_ss, gc_rs,
):
    length = n // 4
    owned = incl.shape[0]
    rows = owned // chunks
    deep = per * rows
    people = resid_ref.shape[0]
    total = float(people * n)
    coding = 32760.0 / math.log(1.0 + LARGEST_TERM * total)
    me = lax.axis_index("ind")
    z = me // 4
    y = (me // 2) % 2
    c = me % 2

    def at(zz, yy, cc):
        return zz * 4 + yy * 2 + cc

    core_dev = {"ind": at(z, y, 1 - c)}
    pair_dev = {"ind": at(z, 1 - y, c)}
    up_dev = {"ind": at(lax.rem(z + 1, length), y, c)}
    down_dev = {"ind": at(lax.rem(z + length - 1, length), y, c)}
    has_up = z < length - 1
    has_down = z > 0

    def remote(src, dst, ss, rs, dev):
        return pltpu.make_async_remote_copy(
            src_ref=src, dst_ref=dst, send_sem=ss, recv_sem=rs,
            device_id=dev, device_id_type=pl.DeviceIdType.MESH,
        )

    def encode(x):
        code = (jnp.log(1.0 + jnp.abs(x)) * coding + 0.5).astype(jnp.int32)
        return jnp.where(x < 0.0, -code, code).astype(jnp.int16)

    def decode(code):
        level = code.astype(jnp.int32).astype(jnp.float32)
        size = jnp.exp(jnp.abs(level) * (1.0 / coding)) - 1.0
        return jnp.where(level < 0.0, -size, size)

    def loop(count, body):
        lax.fori_loop(0, count, lambda i, _: (body(i), 0)[1], 0)

    def for_z(body):
        loop(length, body)

    def place_of(zz, yy, cc):
        return (cc * 2 + yy) * length + zz

    def wide_span(first, count=1):
        return pl.ds(pl.multiple_of(first * deep, math.gcd(deep, 128)), count * deep)

    def span(s, q):
        return pl.ds(pl.multiple_of(q * deep + lax.rem(s, per) * rows, math.gcd(rows, 128)), rows)

    def nth(j):
        return pl.ds(pl.multiple_of(j * rows, math.gcd(rows, 128)), rows)

    def load(g, zz, yy, cc):
        q = place_of(zz, yy, cc)
        return pltpu.make_async_copy(
            geno_hbm.at[:, pl.ds(pl.multiple_of(at(zz, yy, cc) * owned + g * deep, 128), deep)],
            geno.at[g, :, wide_span(q)], geno_sem.at[g, q],
        )

    near = jnp.where(z < length - 1 - z, z, length - 1 - z)
    alone = length - 1 - 2 * near

    def far(j):
        k = j - alone
        side = jnp.where(k % 2 == 0, -1, 1)
        lone = jnp.where(z < length - 1 - z, length - 1 - j, j)
        return jnp.where(j < alone, lone, z + side * (near - k // 2))

    owners = ((1 - y, 1 - c), (1 - y, c), (y, 1 - c), (y, c))

    def load_group(g):
        for yy, cc in owners:
            for_z(lambda i: load(g, i, yy, cc).start())

    barrier = pltpu.get_barrier_semaphore()
    pl.semaphore_signal(barrier, inc=1, device_id=core_dev, device_id_type=pl.DeviceIdType.MESH)
    pl.semaphore_signal(barrier, inc=1, device_id=pair_dev, device_id_type=pl.DeviceIdType.MESH)

    @pl.when(has_up)
    def _():
        pl.semaphore_signal(barrier, inc=1, device_id=up_dev, device_id_type=pl.DeviceIdType.MESH)

    @pl.when(has_down)
    def _():
        pl.semaphore_signal(barrier, inc=1, device_id=down_dev, device_id_type=pl.DeviceIdType.MESH)

    small = [
        pltpu.make_async_copy(incl_hbm, incl, in_sem.at[0]),
        pltpu.make_async_copy(mean_hbm, mean, in_sem.at[1]),
    ]
    sets = chunks // per
    ahead = min(sets, 2)
    loop(ahead, load_group)
    for copy in small:
        copy.start()

    pl.semaphore_wait(barrier, 2 + has_up.astype(jnp.int32) + has_down.astype(jnp.int32))

    eta[...] = jnp.zeros_like(eta)
    scale = scale_ref[...]
    shrink = scale / (1.0 + scale)
    bias = prior_ref[...] - 0.5 * jnp.log1p(scale)
    curve = 0.5 * total * shrink

    def among(s, which):
        found = s < 0
        for k in which:
            found = found | (s == k)
        return found

    def reduce_wide(s):
        return among(s, REDUCE_WIDE)

    def gather_wide(s):
        return among(s, GATHER_WIDE)

    def product(g, yy, cc, out):
        for_z(lambda i: load(g, i, yy, cc).wait())

        def piece(j):
            out[wide_span(4 * j, 4), :] = lax.dot_general(
                geno[g, :, wide_span(place_of(4 * j, yy, cc), 4)], resid_ref[...], (((0,), (0,)), ((), ())),
                preferred_element_type=jnp.float32,
            )

        loop(length // 4, piece)

    def core_copy(g, h):
        return remote(
            core_out.at[lax.rem(g, slots), h], core_in.at[g, h], core_ss.at[g, h], core_rs.at[g, h], core_dev
        )

    def pair_copy(s, j):
        return remote(
            pair_out.at[s, nth(j)], pair_in.at[s, nth(j)], pair_ss.at[s], pair_rs.at[s, j], pair_dev
        )

    def pair_all(s):
        return remote(pair_out.at[s], pair_in.at[s], pair_ss.at[s], pair_rs.at[s, 0], pair_dev)

    def line_copy(s, t, d, f):
        return remote(
            line_out.at[s, t, d, f], line_in.at[s, t, d, f], line_ss.at[s, t, d, f], line_rs.at[s, t, d, f],
            up_dev if d == 0 else down_dev,
        )

    def to_core(g, h, yy):
        @pl.when(g >= slots)
        def _():
            core_copy(g - slots, h).wait_send()

        product(g, yy, 1 - c, core_out.at[lax.rem(g, slots), h])
        core_copy(g, h).start()

    def first_core(g):
        to_core(g, 0, 1 - y)

        @pl.when(g + ahead < sets)
        def _():
            load_group(g + ahead)

    def first_own(g):
        product(g, 1 - y, c, own.at[g, 1])

    def first_pair(g):
        core_copy(g, 0).wait_recv()

        def one(k):
            s = g * per + k

            @pl.when(jnp.logical_not(reduce_wide(s)))
            def _():
                def piece(j):
                    part = span(s, far(j))
                    pair_out[s, nth(j)] = encode(own[g, 1, part] + core_in[g, 0, part])
                    pair_copy(s, j).start()

                for_z(piece)

            @pl.when(reduce_wide(s))
            def _():
                def piece(j):
                    part = span(s, j)
                    own[g, 1, part] = own[g, 1, part] + core_in[g, 0, part]

                for_z(piece)

        loop(per, one)

    def second_core(g):
        to_core(g, 1, y)
        product(g, y, c, own.at[g, 0])

    def second_own(g):
        @pl.when(g == 0)
        def _():
            for copy in small:
                copy.wait()

        core_copy(g, 1).wait_recv()

        def piece(j):
            part = wide_span(4 * j, 4)
            own[g, 0, part] = own[g, 0, part] + core_in[g, 1, part]

        loop(length // 4, piece)

    def from_pair(s, j):
        part = span(s, far(j))
        pair_copy(s, j).wait_recv()
        own[s // per, 0, part] = own[s // per, 0, part] + decode(pair_in[s, nth(j)])

    def line_ends(s, t, wide):
        for d in range(2):
            place = z if d == 0 else length - 1 - z
            block = length - 1 - t if d == 0 else t

            @pl.when(place == 0)
            def _():
                for f in range(2 if wide else 1):
                    line_out[s, t, d, f] = encode(own[s // per, f, span(s, block)])
                    line_copy(s, t, d, f).start()

    def along(s, t, wide):
        for d in range(2):
            place = z if d == 0 else length - 1 - z
            block = length - 1 - t + z if d == 0 else t - (length - 1 - z)

            @pl.when((place > 0) & (place <= t) & (place < length - 1))
            def _():
                for f in range(2 if wide else 1):
                    line_copy(s, t - 1, d, f).wait_recv()
                    line_out[s, t, d, f] = encode(
                        own[s // per, f, span(s, block)] + decode(line_in[s, t - 1, d, f])
                    )
                    line_copy(s, t, d, f).start()

    def arrive(s, wide):
        mine = span(s, z)
        for f in range(2 if wide else 1):
            for d in range(2):
                @pl.when(has_down if d == 0 else has_up)
                def _():
                    line_copy(s, length - 2, d, f).wait_recv()
                    own[s // per, f, mine] = own[s // per, f, mine] + decode(line_in[s, length - 2, d, f])

        if wide:
            pair_out[s, nth(0)] = encode(own[s // per, 1, mine])
            pair_copy(s, 0).start()

    def gz_copy(s, u, d, f):
        k, q = 2 * s + f, span(s, place_of(z - u if d == 0 else z + u, y if f == 0 else 1 - y, c))
        return remote(
            eff.at[s // per, q], eff.at[s // per, q], gz_ss.at[k, u, d], gz_rs.at[k, u, d], up_dev if d == 0 else down_dev
        )

    def gz_landed(s, u, d, f):
        k, q = 2 * s + f, span(s, place_of(z - 1 - u if d == 0 else z + 1 + u, y if f == 0 else 1 - y, c))
        return remote(
            eff.at[s // per, q], eff.at[s // per, q], gz_ss.at[k, u, d], gz_rs.at[k, u, d], up_dev if d == 0 else down_dev
        )

    def gy_copy(s, i, yy):
        q = span(s, place_of(i, yy, c))
        return remote(eff.at[s // per, q], eff.at[s // per, q], gy_ss.at[s], gy_rs.at[s], pair_dev)

    def gc_copy(s, i, yy, cc):
        q = span(s, place_of(i, yy, cc))
        return remote(eff.at[s // per, q], eff.at[s // per, q], gc_ss.at[s], gc_rs.at[s], core_dev)

    def gy_all(s, yy):
        q = wide_span(place_of(0, yy, c), length)
        return remote(eff.at[s, q], eff.at[s, q], gy_ss.at[s], gy_rs.at[s], pair_dev)

    def gc_all(s, first, count):
        q = wide_span(first, count)
        return remote(eff.at[s, q], eff.at[s, q], gc_ss.at[s], gc_rs.at[s], core_dev)

    def use(g, cc):
        def piece(j):
            q = wide_span(place_of(0, 0, cc) + 8 * j, 8)
            eta[...] += jnp.dot(geno[g, :, q], eff[g, q], preferred_element_type=jnp.float32)

        loop(length // 4, piece)

    def send_own(s, f):
        @pl.when(has_up)
        def _():
            gz_copy(s, 0, 0, f).start()

        @pl.when(has_down)
        def _():
            gz_copy(s, 0, 1, f).start()

        gc_copy(s, z, y if f == 0 else 1 - y, c).start()

    def finish(s, wide):
        g, mine = s // per, span(s, z)
        if wide:
            pair_copy(s, 0).wait_recv()
            own[g, 0, mine] = own[g, 0, mine] + decode(pair_in[s, nth(0)])
        here = pl.ds(pl.multiple_of(s * rows, 8), rows)
        before = incl[here, :]
        stat = own[g, 0, mine] / total + before * mean[here, :]
        stat_out[here, :] = stat
        incl_new = 0.5 * before + 0.5 * jax.nn.sigmoid(bias + curve * stat * stat)
        eff[g, span(s, place_of(z, y, c))] = (incl_new * (stat * shrink)).astype(jnp.bfloat16)
        gy_copy(s, z, y).start()
        send_own(s, 0)

    def send_other(s):
        gy_copy(s, z, 1 - y).wait_recv()
        send_own(s, 1)

    def spread(s, u, f, wide):
        for d in range(2):
            source = z - u if d == 0 else z + u

            @pl.when((source >= 0) & (source < length))
            def _():
                gz_landed(s, u - 1, d, f).wait_recv()

                if u < length - 1:
                    @pl.when(has_up if d == 0 else has_down)
                    def _():
                        gz_copy(s, u, d, f).start()

                if not wide:
                    gy_copy(s, source, y).start()

                gc_copy(s, source, y if f == 0 else 1 - y, c).start()

    def last_pair(s):
        gy_all(s, 1 - y).wait_recv()
        gc_all(s, place_of(0, 1 - y, c), length).start()

    def drain(s):
        @pl.when((s % per == 0) & (s // per >= chunks // per - slots))
        def _():
            for h in range(2):
                core_copy(s // per, h).wait_send()

        @pl.when(reduce_wide(s))
        def _():
            pair_copy(s, 0).wait_send()

        @pl.when(jnp.logical_not(reduce_wide(s)))
        def _():
            pair_all(s).wait_send()

        @pl.when(gather_wide(s))
        def _():
            gy_copy(s, z, y).wait_send()

        @pl.when(jnp.logical_not(gather_wide(s)))
        def _():
            gy_all(s, y).wait_send()

        gc_all(s, place_of(0, 0, c), 2 * length).wait_send()

        def step(t):
            for d in range(2):
                place = z if d == 0 else length - 1 - z
                origin = z - t if d == 0 else z + t

                @pl.when((place <= t) & (place < length - 1))
                def _():
                    line_copy(s, t, d, 0).wait_send()

                    @pl.when(reduce_wide(s))
                    def _():
                        line_copy(s, t, d, 1).wait_send()

                @pl.when((origin >= 0) & (origin < length) & (place < length - 1))
                def _():
                    gz_copy(s, t, d, 0).wait_send()

                    @pl.when(gather_wide(s))
                    def _():
                        gz_copy(s, t, d, 1).wait_send()

        loop(length - 1, step)

    def use_own(g):
        use(g, c)

    def use_core(g):
        gc_all(g, place_of(0, 0, 1 - c), 2 * length).wait_recv()
        use(g, 1 - c)
        drain(g)

    groups = {
        "P0": first_core, "P1": first_own, "P2": first_pair, "P3": second_core, "P4": second_own,
        "U1": use_own, "U2": use_core,
    }
    tasks = {"OT": (gather_wide, True, send_other), "LA": (gather_wide, False, last_pair)}
    for j in range(length):
        tasks[f"D{j}Y"] = (reduce_wide, False, functools.partial(from_pair, j=j))
    for kind in "YZ":
        wide = kind == "Z"
        for t in range(length - 1):
            tasks[f"E{t}{kind}"] = (reduce_wide, wide, functools.partial(line_ends, t=t, wide=wide))
            if t > 0:
                tasks[f"T{t}{kind}"] = (reduce_wide, wide, functools.partial(along, t=t, wide=wide))
        tasks["AR" + kind] = (reduce_wide, wide, functools.partial(arrive, wide=wide))
        tasks["FI" + kind] = (reduce_wide, wide, functools.partial(finish, wide=wide))
        for u in range(1, length):
            tasks[f"g{u}{kind}"] = (gather_wide, wide, functools.partial(spread, u=u, f=0, wide=wide))
            if wide:
                tasks[f"h{u}Z"] = (gather_wide, True, functools.partial(spread, u=u, f=1, wide=True))

    steps = plan(length)
    names = [*groups, *tasks]
    least = min(math.floor(steps[name]) for name in names)
    late = {name: math.floor(steps[name]) - least for name in names}
    order = sorted(names, key=lambda name: steps[name] - math.floor(steps[name]))

    def wave(w):
        for name in order:
            s = w - late[name]
            go = (s >= 0) & (s < chunks)
            if name in groups:
                @pl.when(go & (s % per == 0))
                def _():
                    groups[name](s // per)
            else:
                test, wanted, body = tasks[name]

                @pl.when(go & (test(s) if wanted else jnp.logical_not(test(s))))
                def _():
                    body(s)

    loop(chunks + max(late.values()), wave)


def outputs_kernel(
    half_total, stat_ref, incl_ref, eta_ref, labels_ref, prior_ref, scale_ref, offset_ref,
    incl_out, mean_out, resid_out,
):
    scale = scale_ref[...]
    shrink = scale / (1.0 + scale)
    bias = prior_ref[...] - 0.5 * jnp.log1p(scale)
    stat = stat_ref[...]
    mean_out[...] = stat * shrink
    logit = bias + (half_total * shrink) * stat * stat
    incl_out[...] = 0.5 * incl_ref[...] + 0.5 * jax.nn.sigmoid(logit)
    resid_out[...] = 4.0 * (
        labels_ref[...].astype(jnp.float32) - jax.nn.sigmoid(eta_ref[...] + offset_ref[...])
    )


def on_device(genotype, residual, labels, incl_old, mean_old, prior_logit, slab_scale, offset):
    n = lax.axis_size("ind")
    people, _ = genotype.shape
    owned, columns = incl_old.shape
    length = n // 4
    per = 1
    chunks = per * max(1, min(8, owned // 128))
    sets = chunks // per
    slots = max(1, min(sets // 2, 3))
    rows = owned // chunks
    f32, bf16, i16 = jnp.float32, jnp.bfloat16, jnp.int16
    anywhere = pl.BlockSpec(memory_space=pl.ANY)
    vmem = pl.BlockSpec(memory_space=pltpu.VMEM)
    dma = pltpu.SemaphoreType.DMA
    hops = length - 1
    prior, scale, shift = (v.reshape(1, -1) for v in (prior_logit, slab_scale, offset))
    stat, eta = pl.pallas_call(
        functools.partial(sweep_kernel, n, chunks, per, slots),
        out_shape=(
            jax.ShapeDtypeStruct((owned, columns), f32),
            jax.ShapeDtypeStruct((people, columns), f32),
        ),
        in_specs=[anywhere, vmem, anywhere, anywhere, vmem, vmem],
        out_specs=(vmem, vmem),
        scratch_shapes=[
            pltpu.VMEM((sets, people, n * per * rows), bf16),
            pltpu.VMEM(incl_old.shape, f32),
            pltpu.VMEM(mean_old.shape, f32),
            pltpu.VMEM((slots, 2, length * per * rows, columns), f32),
            pltpu.VMEM((sets, 2, length * per * rows, columns), f32),
            pltpu.VMEM((chunks, length * rows, columns), i16),
            pltpu.VMEM((chunks, length * rows, columns), i16),
            pltpu.VMEM((sets, 2, length * per * rows, columns), f32),
            pltpu.VMEM((chunks, hops, 2, 2, rows, columns), i16),
            pltpu.VMEM((chunks, hops, 2, 2, rows, columns), i16),
            pltpu.VMEM((sets, n * per * rows, columns), bf16),
            dma((sets, n)),
            dma((2,)),
            dma((sets, 2)),
            dma((sets, 2)),
            dma((chunks,)),
            dma((chunks, length)),
            dma((chunks, hops, 2, 2)),
            dma((chunks, hops, 2, 2)),
            dma((2 * chunks, hops, 2)),
            dma((2 * chunks, hops, 2)),
            dma((chunks,)),
            dma((chunks,)),
            dma((chunks,)),
            dma((chunks,)),
        ],
        compiler_params=pltpu.CompilerParams(
            collective_id=0, has_side_effects=True, vmem_limit_bytes=67043328
        ),
        name="sweep",
    )(genotype, residual, incl_old, mean_old, prior, scale)

    steps = 2 if owned % 32 == 0 and people % 32 == 0 else 1
    upper = pl.BlockSpec((owned // steps, columns), lambda i: (i, 0))
    lower = pl.BlockSpec((people // steps, columns), lambda i: (i, 0))
    flat = pl.BlockSpec((1, columns), lambda i: (0, 0))
    return pl.pallas_call(
        functools.partial(outputs_kernel, 0.5 * people * n),
        grid=(steps,),
        out_shape=(
            jax.ShapeDtypeStruct((owned, columns), f32),
            jax.ShapeDtypeStruct((owned, columns), f32),
            jax.ShapeDtypeStruct((people, columns), f32),
        ),
        in_specs=[upper, upper, lower, lower, flat, flat, flat],
        out_specs=(upper, upper, lower),
        name="outputs",
    )(stat, incl_old, eta, labels, prior, scale, shift)


def solution(mesh):
    placed = (
        P(("groups", "ind"), None),
        P(("groups", "ind"), None),
        P(("groups", "ind"), None),
        P(("groups", "ind"), None),
        P(("groups", "ind"), None),
        P(),
        P(),
        P(),
    )
    return jax.shard_map(
        on_device,
        mesh=mesh,
        in_specs=placed,
        out_specs=(
            P(("groups", "ind"), None),
            P(("groups", "ind"), None),
            P(("groups", "ind"), None),
        ),
        check_vma=False,
    )
```

```python
import functools
import math

import jax
import jax.numpy as jnp
from jax import lax
from jax.experimental import pallas as pl
from jax.experimental.pallas import tpu as pltpu
from jax.sharding import PartitionSpec as P

LARGEST_TERM = 64.0

REDUCE_WIDE = (0, 3, 7,)
GATHER_WIDE = (2, 6, 7,)
PLAN = {
    "P0": 13.357, "P1": 13.631, "P3": 13.740, "P2": 14.320, "P4": 14.522, "E0Z": 14.526, "E1Z": 15.600,
    "D0Y": 16.146, "D1Y": 16.150, "E0Y": 16.150, "T1Z": 16.216, "E2Z": 16.515, "E1Y": 17.469,
    "T1Y": 17.615, "T2Z": 17.688, "D2Y": 17.728, "E2Y": 18.501, "ARZ": 18.788, "T2Y": 19.069,
    "D3Y": 19.966, "ARY": 20.081, "FIY": 20.098, "FIZ": 20.170, "g1Z": 21.204, "g1Y": 21.855,
    "g2Z": 22.258, "g2Y": 22.911, "OT": 23.318, "g3Z": 23.621, "g3Y": 24.145, "h1Z": 26.220,
    "LAZ": 26.437, "LA": 26.522, "U1": 27.343, "U2": 27.730,
}


def plan(length):
    if length == 4:
        return PLAN
    steps = {"P0": -3.0, "P1": -2.9, "P2": -2.8, "P3": -2.7, "P4": -2.6}
    for t in range(length):
        steps[f"D{t}Y"] = 0.5 + 0.01 * t
    for k in "YZ":
        for t in range(length - 1):
            steps[f"E{t}{k}"] = steps[f"T{t}{k}"] = t + 0.9 - 0.02 * t
        steps["AR" + k] = length + 0.5
        steps["FI" + k] = length + 1.4
        for u in range(1, length):
            steps[f"g{u}{k}"] = length + 1 + u + 0.35 - 0.02 * u
    steps["OT"] = length + 2.36
    steps["h1Z"] = length + 3.34
    steps["LA"] = 2 * length + 2.9
    steps["LAZ"] = 2 * length + 2.91
    steps["U1"] = 2 * length + 4.92
    steps["U2"] = 2 * length + 5.95
    return steps


def sweep_kernel(
    n, chunks, per, slots,
    geno_hbm, resid_ref, incl_hbm, mean_hbm, prior_ref, scale_ref,
    stat_out, eta,
    geno, incl, mean, core_out, core_in, pair_out, pair_in, own, line_out, line_in, eff,
    geno_sem, in_sem, core_ss, core_rs, pair_ss, pair_rs, line_ss, line_rs,
    gz_ss, gz_rs, gy_ss, gy_rs, gc_ss, gc_rs,
):
    length = n // 4
    owned = incl.shape[0]
    rows = owned // chunks
    deep = per * rows
    people = resid_ref.shape[0]
    total = float(people * n)
    coding = 32760.0 / math.log(1.0 + LARGEST_TERM * total)
    me = lax.axis_index("ind")
    z = me // 4
    y = (me // 2) % 2
    c = me % 2

    def at(zz, yy, cc):
        return zz * 4 + yy * 2 + cc

    core_dev = {"ind": at(z, y, 1 - c)}
    pair_dev = {"ind": at(z, 1 - y, c)}
    up_dev = {"ind": at(lax.rem(z + 1, length), y, c)}
    down_dev = {"ind": at(lax.rem(z + length - 1, length), y, c)}
    has_up = z < length - 1
    even = z % 2 == 0
    mate = z + 1 - 2 * (z % 2)
    has_down = z > 0

    def remote(src, dst, ss, rs, dev):
        return pltpu.make_async_remote_copy(
            src_ref=src, dst_ref=dst, send_sem=ss, recv_sem=rs,
            device_id=dev, device_id_type=pl.DeviceIdType.MESH,
        )

    def encode(x):
        code = (jnp.log(1.0 + jnp.abs(x)) * coding + 0.5).astype(jnp.int32)
        return jnp.where(x < 0.0, -code, code).astype(jnp.int16)

    def decode(code):
        level = code.astype(jnp.int32).astype(jnp.float32)
        size = jnp.exp(jnp.abs(level) * (1.0 / coding)) - 1.0
        return jnp.where(level < 0.0, -size, size)

    def loop(count, body):
        lax.fori_loop(0, count, lambda i, _: (body(i), 0)[1], 0)

    def for_z(body):
        loop(length, body)

    def place_of(zz, yy, cc):
        return (cc * 2 + yy) * length + zz

    def wide_span(first, count=1):
        return pl.ds(pl.multiple_of(first * deep, math.gcd(deep, 128)), count * deep)

    def span(s, q):
        return pl.ds(pl.multiple_of(q * deep + lax.rem(s, per) * rows, math.gcd(rows, 128)), rows)

    def nth(j):
        return pl.ds(pl.multiple_of(j * rows, math.gcd(rows, 128)), rows)

    def load(g, zz, yy, cc):
        q = place_of(zz, yy, cc)
        return pltpu.make_async_copy(
            geno_hbm.at[:, pl.ds(pl.multiple_of(at(zz, yy, cc) * owned + g * deep, 128), deep)],
            geno.at[g, :, wide_span(q)], geno_sem.at[g, q],
        )

    near = jnp.where(z < length - 1 - z, z, length - 1 - z)
    alone = length - 1 - 2 * near

    def far(j):
        k = j - alone
        side = jnp.where(k % 2 == 0, -1, 1)
        lone = jnp.where(z < length - 1 - z, length - 1 - j, j)
        return jnp.where(j < alone, lone, z + side * (near - k // 2))

    owners = ((1 - y, 1 - c), (1 - y, c), (y, 1 - c), (y, c))

    def load_group(g):
        for yy, cc in owners:
            for_z(lambda i: load(g, i, yy, cc).start())

    barrier = pltpu.get_barrier_semaphore()
    pl.semaphore_signal(barrier, inc=1, device_id=core_dev, device_id_type=pl.DeviceIdType.MESH)
    pl.semaphore_signal(barrier, inc=1, device_id=pair_dev, device_id_type=pl.DeviceIdType.MESH)

    @pl.when(has_up)
    def _():
        pl.semaphore_signal(barrier, inc=1, device_id=up_dev, device_id_type=pl.DeviceIdType.MESH)

    @pl.when(has_down)
    def _():
        pl.semaphore_signal(barrier, inc=1, device_id=down_dev, device_id_type=pl.DeviceIdType.MESH)

    small = [
        pltpu.make_async_copy(incl_hbm, incl, in_sem.at[0]),
        pltpu.make_async_copy(mean_hbm, mean, in_sem.at[1]),
    ]
    sets = chunks // per
    ahead = min(sets, 2)
    loop(ahead, load_group)
    for copy in small:
        copy.start()

    pl.semaphore_wait(barrier, 2 + has_up.astype(jnp.int32) + has_down.astype(jnp.int32))

    eta[...] = jnp.zeros_like(eta)
    scale = scale_ref[...]
    shrink = scale / (1.0 + scale)
    bias = prior_ref[...] - 0.5 * jnp.log1p(scale)
    curve = 0.5 * total * shrink

    def among(s, which):
        found = s < 0
        for k in which:
            found = found | (s == k)
        return found

    def reduce_wide(s):
        return among(s, REDUCE_WIDE)

    def gather_wide(s):
        return among(s, GATHER_WIDE)

    def product(g, yy, cc, out):
        for_z(lambda i: load(g, i, yy, cc).wait())

        def piece(j):
            out[wide_span(4 * j, 4), :] = lax.dot_general(
                geno[g, :, wide_span(place_of(4 * j, yy, cc), 4)], resid_ref[...], (((0,), (0,)), ((), ())),
                preferred_element_type=jnp.float32,
            )

        loop(length // 4, piece)

    def core_copy(g, h):
        return remote(
            core_out.at[lax.rem(g, slots), h], core_in.at[g, h], core_ss.at[g, h], core_rs.at[g, h], core_dev
        )

    def pair_copy(s, j):
        return remote(
            pair_out.at[s, nth(j)], pair_in.at[s, nth(j)], pair_ss.at[s], pair_rs.at[s, j], pair_dev
        )

    def pair_all(s):
        return remote(pair_out.at[s], pair_in.at[s], pair_ss.at[s], pair_rs.at[s, 0], pair_dev)

    def line_copy(s, t, d, f):
        return remote(
            line_out.at[s, t, d, f], line_in.at[s, t, d, f], line_ss.at[s, t, d, f], line_rs.at[s, t, d, f],
            up_dev if d == 0 else down_dev,
        )

    def to_core(g, h, yy):
        @pl.when(g >= slots)
        def _():
            core_copy(g - slots, h).wait_send()

        product(g, yy, 1 - c, core_out.at[lax.rem(g, slots), h])
        core_copy(g, h).start()

    def first_core(g):
        to_core(g, 0, 1 - y)

        @pl.when(g + ahead < sets)
        def _():
            load_group(g + ahead)

    def first_own(g):
        product(g, 1 - y, c, own.at[g, 1])

    def first_pair(g):
        core_copy(g, 0).wait_recv()

        def one(k):
            s = g * per + k

            @pl.when(jnp.logical_not(reduce_wide(s)))
            def _():
                def piece(j):
                    part = span(s, far(j))
                    pair_out[s, nth(j)] = encode(own[g, 1, part] + core_in[g, 0, part])
                    pair_copy(s, j).start()

                for_z(piece)

            @pl.when(reduce_wide(s))
            def _():
                def piece(j):
                    part = span(s, j)
                    own[g, 1, part] = own[g, 1, part] + core_in[g, 0, part]

                for_z(piece)

        loop(per, one)

    def second_core(g):
        to_core(g, 1, y)
        product(g, y, c, own.at[g, 0])

    def second_own(g):
        @pl.when(g == 0)
        def _():
            for copy in small:
                copy.wait()

        core_copy(g, 1).wait_recv()

        def piece(j):
            part = wide_span(4 * j, 4)
            own[g, 0, part] = own[g, 0, part] + core_in[g, 1, part]

        loop(length // 4, piece)

    def from_pair(s, j):
        part = span(s, far(j))
        pair_copy(s, j).wait_recv()
        own[s // per, 0, part] = own[s // per, 0, part] + decode(pair_in[s, nth(j)])

    def line_ends(s, t, wide):
        for d in range(2):
            place = z if d == 0 else length - 1 - z
            block = length - 1 - t if d == 0 else t

            @pl.when(place == 0)
            def _():
                for f in range(2 if wide else 1):
                    line_out[s, t, d, f] = encode(own[s // per, f, span(s, block)])
                    line_copy(s, t, d, f).start()

    def along(s, t, wide):
        for d in range(2):
            place = z if d == 0 else length - 1 - z
            block = length - 1 - t + z if d == 0 else t - (length - 1 - z)

            @pl.when((place > 0) & (place <= t) & (place < length - 1))
            def _():
                for f in range(2 if wide else 1):
                    line_copy(s, t - 1, d, f).wait_recv()
                    line_out[s, t, d, f] = encode(
                        own[s // per, f, span(s, block)] + decode(line_in[s, t - 1, d, f])
                    )
                    line_copy(s, t, d, f).start()

    def arrive(s, wide):
        mine = span(s, z)
        for f in range(2 if wide else 1):
            for d in range(2):
                @pl.when(has_down if d == 0 else has_up)
                def _():
                    line_copy(s, length - 2, d, f).wait_recv()
                    own[s // per, f, mine] = own[s // per, f, mine] + decode(line_in[s, length - 2, d, f])

        if wide:
            pair_out[s, nth(0)] = encode(own[s // per, 1, mine])
            pair_copy(s, 0).start()

    def gz_copy(s, u, d, f):
        k, q = 2 * s + f, span(s, place_of(z - u if d == 0 else z + u, y if f == 0 else 1 - y, c))
        return remote(
            eff.at[s // per, q], eff.at[s // per, q], gz_ss.at[k, u, d], gz_rs.at[k, u, d], up_dev if d == 0 else down_dev
        )

    def gz_landed(s, u, d, f):
        k, q = 2 * s + f, span(s, place_of(z - 1 - u if d == 0 else z + 1 + u, y if f == 0 else 1 - y, c))
        return remote(
            eff.at[s // per, q], eff.at[s // per, q], gz_ss.at[k, u, d], gz_rs.at[k, u, d], up_dev if d == 0 else down_dev
        )

    def gy_copy(s, i, yy):
        q = span(s, place_of(i, yy, c))
        return remote(eff.at[s // per, q], eff.at[s // per, q], gy_ss.at[s], gy_rs.at[s, i], pair_dev)

    def gc_copy(s, i, yy, cc):
        q = span(s, place_of(i, yy, cc))
        return remote(eff.at[s // per, q], eff.at[s // per, q], gc_ss.at[s], gc_rs.at[s], core_dev)

    def gy_sent(s, count):
        q = wide_span(0, count)
        return remote(eff.at[s, q], eff.at[s, q], gy_ss.at[s], gy_rs.at[s, 0], pair_dev)

    def gc_all(s, first, count):
        q = wide_span(first, count)
        return remote(eff.at[s, q], eff.at[s, q], gc_ss.at[s], gc_rs.at[s], core_dev)

    def use(g, cc):
        def piece(j):
            q = wide_span(place_of(0, 0, cc) + 8 * j, 8)
            eta[...] += jnp.dot(geno[g, :, q], eff[g, q], preferred_element_type=jnp.float32)

        loop(length // 4, piece)

    def send_own(s, f):
        @pl.when(has_up)
        def _():
            gz_copy(s, 0, 0, f).start()

        @pl.when(has_down)
        def _():
            gz_copy(s, 0, 1, f).start()

        gc_copy(s, z, y if f == 0 else 1 - y, c).start()

    def finish(s, wide):
        g, mine = s // per, span(s, z)
        if wide:
            pair_copy(s, 0).wait_recv()
            own[g, 0, mine] = own[g, 0, mine] + decode(pair_in[s, nth(0)])
        here = pl.ds(pl.multiple_of(s * rows, 8), rows)
        before = incl[here, :]
        stat = own[g, 0, mine] / total + before * mean[here, :]
        stat_out[here, :] = stat
        incl_new = 0.5 * before + 0.5 * jax.nn.sigmoid(bias + curve * stat * stat)
        eff[g, span(s, place_of(z, y, c))] = (incl_new * (stat * shrink)).astype(jnp.bfloat16)
        gy_copy(s, z, y).start()
        send_own(s, 0)

    def send_other(s):
        gy_copy(s, z, 1 - y).wait_recv()

        @pl.when(even)
        def _():
            gz_copy(s, 0, 0, 1).start()

        @pl.when(jnp.logical_not(even))
        def _():
            gz_copy(s, 0, 1, 1).start()

        gc_copy(s, z, 1 - y, c).start()

    def take_other(s):
        @pl.when(even)
        def _():
            gz_landed(s, 0, 1, 1).wait_recv()

        @pl.when(jnp.logical_not(even))
        def _():
            gz_landed(s, 0, 0, 1).wait_recv()

        gc_copy(s, mate, 1 - y, c).start()

    def spread(s, u, f, wide):
        for d in range(2):
            source = z - u if d == 0 else z + u

            @pl.when((source >= 0) & (source < length))
            def _():
                gz_landed(s, u - 1, d, f).wait_recv()

                if u < length - 1:
                    @pl.when(has_up if d == 0 else has_down)
                    def _():
                        gz_copy(s, u, d, f).start()

                if wide and u == 1:
                    @pl.when(source != mate)
                    def _():
                        gy_copy(s, source, y).start()
                else:
                    gy_copy(s, source, y).start()

                gc_copy(s, source, y if f == 0 else 1 - y, c).start()

    def last_pair(s):
        for_z(lambda i: gy_copy(s, i, 1 - y).wait_recv())
        gc_all(s, place_of(0, 1 - y, c), length).start()

    def last_others(s):
        def take(i):
            @pl.when((i != z) & (i != mate))
            def _():
                gy_copy(s, i, 1 - y).wait_recv()
                gc_copy(s, i, 1 - y, c).start()

        for_z(take)

    def drain(s):
        @pl.when((s % per == 0) & (s // per >= chunks // per - slots))
        def _():
            for h in range(2):
                core_copy(s // per, h).wait_send()

        @pl.when(reduce_wide(s))
        def _():
            pair_copy(s, 0).wait_send()

        @pl.when(jnp.logical_not(reduce_wide(s)))
        def _():
            pair_all(s).wait_send()

        @pl.when(gather_wide(s))
        def _():
            gy_sent(s, length - 1).wait_send()

            @pl.when(even)
            def _():
                gz_copy(s, 0, 0, 1).wait_send()

            @pl.when(jnp.logical_not(even))
            def _():
                gz_copy(s, 0, 1, 1).wait_send()

        @pl.when(jnp.logical_not(gather_wide(s)))
        def _():
            gy_sent(s, length).wait_send()

        gc_all(s, place_of(0, 0, c), 2 * length).wait_send()

        def step(t):
            for d in range(2):
                place = z if d == 0 else length - 1 - z
                origin = z - t if d == 0 else z + t

                @pl.when((place <= t) & (place < length - 1))
                def _():
                    line_copy(s, t, d, 0).wait_send()

                    @pl.when(reduce_wide(s))
                    def _():
                        line_copy(s, t, d, 1).wait_send()

                @pl.when((origin >= 0) & (origin < length) & (place < length - 1))
                def _():
                    gz_copy(s, t, d, 0).wait_send()

        loop(length - 1, step)

    def use_own(g):
        use(g, c)

    def use_core(g):
        gc_all(g, place_of(0, 0, 1 - c), 2 * length).wait_recv()
        use(g, 1 - c)
        drain(g)

    groups = {
        "P0": first_core, "P1": first_own, "P2": first_pair, "P3": second_core, "P4": second_own,
        "U1": use_own, "U2": use_core,
    }
    tasks = {
        "OT": (gather_wide, True, send_other), "h1Z": (gather_wide, True, take_other),
        "LA": (gather_wide, False, last_pair), "LAZ": (gather_wide, True, last_others),
    }
    for j in range(length):
        tasks[f"D{j}Y"] = (reduce_wide, False, functools.partial(from_pair, j=j))
    for kind in "YZ":
        wide = kind == "Z"
        for t in range(length - 1):
            tasks[f"E{t}{kind}"] = (reduce_wide, wide, functools.partial(line_ends, t=t, wide=wide))
            if t > 0:
                tasks[f"T{t}{kind}"] = (reduce_wide, wide, functools.partial(along, t=t, wide=wide))
        tasks["AR" + kind] = (reduce_wide, wide, functools.partial(arrive, wide=wide))
        tasks["FI" + kind] = (reduce_wide, wide, functools.partial(finish, wide=wide))
        for u in range(1, length):
            tasks[f"g{u}{kind}"] = (gather_wide, wide, functools.partial(spread, u=u, f=0, wide=wide))

    steps = plan(length)
    names = [*groups, *tasks]
    least = min(math.floor(steps[name]) for name in names)
    late = {name: math.floor(steps[name]) - least for name in names}
    order = sorted(names, key=lambda name: steps[name] - math.floor(steps[name]))

    def wave(w):
        for name in order:
            s = w - late[name]
            go = (s >= 0) & (s < chunks)
            if name in groups:
                @pl.when(go & (s % per == 0))
                def _():
                    groups[name](s // per)
            else:
                test, wanted, body = tasks[name]

                @pl.when(go & (test(s) if wanted else jnp.logical_not(test(s))))
                def _():
                    body(s)

    loop(chunks + max(late.values()), wave)


def outputs_kernel(
    half_total, stat_ref, incl_ref, eta_ref, labels_ref, prior_ref, scale_ref, offset_ref,
    incl_out, mean_out, resid_out,
):
    scale = scale_ref[...]
    shrink = scale / (1.0 + scale)
    bias = prior_ref[...] - 0.5 * jnp.log1p(scale)
    stat = stat_ref[...]
    mean_out[...] = stat * shrink
    logit = bias + (half_total * shrink) * stat * stat
    incl_out[...] = 0.5 * incl_ref[...] + 0.5 * jax.nn.sigmoid(logit)
    resid_out[...] = 4.0 * (
        labels_ref[...].astype(jnp.float32) - jax.nn.sigmoid(eta_ref[...] + offset_ref[...])
    )


def on_device(genotype, residual, labels, incl_old, mean_old, prior_logit, slab_scale, offset):
    n = lax.axis_size("ind")
    people, _ = genotype.shape
    owned, columns = incl_old.shape
    length = n // 4
    per = 1
    chunks = per * max(1, min(8, owned // 128))
    sets = chunks // per
    slots = max(1, min(sets // 2, 3))
    rows = owned // chunks
    f32, bf16, i16 = jnp.float32, jnp.bfloat16, jnp.int16
    anywhere = pl.BlockSpec(memory_space=pl.ANY)
    vmem = pl.BlockSpec(memory_space=pltpu.VMEM)
    dma = pltpu.SemaphoreType.DMA
    hops = length - 1
    prior, scale, shift = (v.reshape(1, -1) for v in (prior_logit, slab_scale, offset))
    stat, eta = pl.pallas_call(
        functools.partial(sweep_kernel, n, chunks, per, slots),
        out_shape=(
            jax.ShapeDtypeStruct((owned, columns), f32),
            jax.ShapeDtypeStruct((people, columns), f32),
        ),
        in_specs=[anywhere, vmem, anywhere, anywhere, vmem, vmem],
        out_specs=(vmem, vmem),
        scratch_shapes=[
            pltpu.VMEM((sets, people, n * per * rows), bf16),
            pltpu.VMEM(incl_old.shape, f32),
            pltpu.VMEM(mean_old.shape, f32),
            pltpu.VMEM((slots, 2, length * per * rows, columns), f32),
            pltpu.VMEM((sets, 2, length * per * rows, columns), f32),
            pltpu.VMEM((chunks, length * rows, columns), i16),
            pltpu.VMEM((chunks, length * rows, columns), i16),
            pltpu.VMEM((sets, 2, length * per * rows, columns), f32),
            pltpu.VMEM((chunks, hops, 2, 2, rows, columns), i16),
            pltpu.VMEM((chunks, hops, 2, 2, rows, columns), i16),
            pltpu.VMEM((sets, n * per * rows, columns), bf16),
            dma((sets, n)),
            dma((2,)),
            dma((sets, 2)),
            dma((sets, 2)),
            dma((chunks,)),
            dma((chunks, length)),
            dma((chunks, hops, 2, 2)),
            dma((chunks, hops, 2, 2)),
            dma((2 * chunks, hops, 2)),
            dma((2 * chunks, hops, 2)),
            dma((chunks,)),
            dma((chunks, length)),
            dma((chunks,)),
            dma((chunks,)),
        ],
        compiler_params=pltpu.CompilerParams(
            collective_id=0, has_side_effects=True, vmem_limit_bytes=67043328
        ),
        name="sweep",
    )(genotype, residual, incl_old, mean_old, prior, scale)

    steps = 2 if owned % 32 == 0 and people % 32 == 0 else 1
    upper = pl.BlockSpec((owned // steps, columns), lambda i: (i, 0))
    lower = pl.BlockSpec((people // steps, columns), lambda i: (i, 0))
    flat = pl.BlockSpec((1, columns), lambda i: (0, 0))
    return pl.pallas_call(
        functools.partial(outputs_kernel, 0.5 * people * n),
        grid=(steps,),
        out_shape=(
            jax.ShapeDtypeStruct((owned, columns), f32),
            jax.ShapeDtypeStruct((owned, columns), f32),
            jax.ShapeDtypeStruct((people, columns), f32),
        ),
        in_specs=[upper, upper, lower, lower, flat, flat, flat],
        out_specs=(upper, upper, lower),
        name="outputs",
    )(stat, incl_old, eta, labels, prior, scale, shift)


def solution(mesh):
    placed = (
        P(("groups", "ind"), None),
        P(("groups", "ind"), None),
        P(("groups", "ind"), None),
        P(("groups", "ind"), None),
        P(("groups", "ind"), None),
        P(),
        P(),
        P(),
    )
    return jax.shard_map(
        on_device,
        mesh=mesh,
        in_specs=placed,
        out_specs=(
            P(("groups", "ind"), None),
            P(("groups", "ind"), None),
            P(("groups", "ind"), None),
        ),
        check_vma=False,
    )
```

```python
import functools
import math

import jax
import jax.numpy as jnp
from jax import lax
from jax.experimental import pallas as pl
from jax.experimental.pallas import tpu as pltpu
from jax.sharding import PartitionSpec as P

LARGEST_TERM = 64.0

REDUCE_WIDE = (0, 3, 7,)
GATHER_WIDE = (2, 6, 7,)
PLAN = {
    "P0": 13.357, "P1": 13.631, "P3": 13.740, "P2": 14.320, "P4": 14.522, "E0Z": 14.526, "E1Z": 15.600,
    "D0Y": 16.146, "D1Y": 16.150, "E0Y": 16.150, "T1Z": 16.216, "E2Z": 16.515, "E1Y": 17.469,
    "T1Y": 17.615, "T2Z": 17.688, "D2Y": 17.728, "E2Y": 18.501, "ARZ": 18.788, "T2Y": 19.069,
    "D3Y": 19.966, "ARY": 20.081, "FIY": 20.098, "FIZ": 20.170, "g1Z": 21.204, "g1Y": 21.855,
    "g2Z": 22.258, "g2Y": 22.911, "OT": 23.318, "g3Z": 23.621, "g3Y": 24.145, "h1Z": 26.220,
    "LAZ": 26.437, "LA": 26.522, "U1": 27.343, "U2": 27.730,
}


def plan(length):
    if length == 4:
        return PLAN
    steps = {"P0": -3.0, "P1": -2.9, "P2": -2.8, "P3": -2.7, "P4": -2.6}
    for t in range(length):
        steps[f"D{t}Y"] = 0.5 + 0.01 * t
    for k in "YZ":
        for t in range(length - 1):
            steps[f"E{t}{k}"] = steps[f"T{t}{k}"] = t + 0.9 - 0.02 * t
        steps["AR" + k] = length + 0.5
        steps["FI" + k] = length + 1.4
        for u in range(1, length):
            steps[f"g{u}{k}"] = length + 1 + u + 0.35 - 0.02 * u
    steps["OT"] = length + 2.36
    steps["h1Z"] = length + 3.34
    steps["LA"] = 2 * length + 2.9
    steps["LAZ"] = 2 * length + 2.91
    steps["U1"] = 2 * length + 4.92
    steps["U2"] = 2 * length + 5.95
    return steps


def sweep_kernel(
    n, chunks, per, slots,
    geno_hbm, resid_ref, incl_hbm, mean_hbm, prior_ref, scale_ref,
    stat_out, eta,
    geno, incl, mean, core_out, core_in, pair_out, pair_in, own, line_out, line_in, eff,
    geno_sem, in_sem, core_ss, core_rs, pair_ss, pair_rs, line_ss, line_rs,
    gz_ss, gz_rs, gy_ss, gy_rs, gc_ss, gc_rs,
):
    length = n // 4
    owned = incl.shape[0]
    rows = owned // chunks
    deep = per * rows
    people = resid_ref.shape[0]
    total = float(people * n)
    coding = 32760.0 / math.log(1.0 + LARGEST_TERM * total)
    me = lax.axis_index("ind")
    z = me // 4
    y = (me // 2) % 2
    c = me % 2

    def at(zz, yy, cc):
        return zz * 4 + yy * 2 + cc

    core_dev = {"ind": at(z, y, 1 - c)}
    pair_dev = {"ind": at(z, 1 - y, c)}
    up_dev = {"ind": at(lax.rem(z + 1, length), y, c)}
    down_dev = {"ind": at(lax.rem(z + length - 1, length), y, c)}
    has_up = z < length - 1
    even = z % 2 == 0
    mate = z + 1 - 2 * (z % 2)
    has_down = z > 0

    def remote(src, dst, ss, rs, dev):
        return pltpu.make_async_remote_copy(
            src_ref=src, dst_ref=dst, send_sem=ss, recv_sem=rs,
            device_id=dev, device_id_type=pl.DeviceIdType.MESH,
        )

    def encode(x):
        code = (jnp.log(1.0 + jnp.abs(x)) * coding + 0.5).astype(jnp.int32)
        return jnp.where(x < 0.0, -code, code).astype(jnp.int16)

    def decode(code):
        level = code.astype(jnp.int32).astype(jnp.float32)
        size = jnp.exp(jnp.abs(level) * (1.0 / coding)) - 1.0
        return jnp.where(level < 0.0, -size, size)

    def loop(count, body):
        lax.fori_loop(0, count, lambda i, _: (body(i), 0)[1], 0)

    def for_z(body):
        loop(length, body)

    def place_of(zz, yy, cc):
        return (cc * 2 + yy) * length + zz

    def wide_span(first, count=1):
        return pl.ds(pl.multiple_of(first * deep, math.gcd(deep, 128)), count * deep)

    def span(s, q):
        return pl.ds(pl.multiple_of(q * deep + lax.rem(s, per) * rows, math.gcd(rows, 128)), rows)

    def nth(j):
        return pl.ds(pl.multiple_of(j * rows, math.gcd(rows, 128)), rows)

    def load(g, zz, yy, cc):
        q = place_of(zz, yy, cc)
        return pltpu.make_async_copy(
            geno_hbm.at[:, pl.ds(pl.multiple_of(at(zz, yy, cc) * owned + g * deep, 128), deep)],
            geno.at[g, :, wide_span(q)], geno_sem.at[g, q],
        )

    near = jnp.where(z < length - 1 - z, z, length - 1 - z)
    alone = length - 1 - 2 * near

    def far(j):
        k = j - alone
        side = jnp.where(k % 2 == 0, -1, 1)
        lone = jnp.where(z < length - 1 - z, length - 1 - j, j)
        return jnp.where(j < alone, lone, z + side * (near - k // 2))

    owners = ((1 - y, 1 - c), (1 - y, c), (y, 1 - c), (y, c))

    def load_group(g):
        for yy, cc in owners:
            for_z(lambda i: load(g, i, yy, cc).start())

    barrier = pltpu.get_barrier_semaphore()
    pl.semaphore_signal(barrier, inc=1, device_id=core_dev, device_id_type=pl.DeviceIdType.MESH)
    pl.semaphore_signal(barrier, inc=1, device_id=pair_dev, device_id_type=pl.DeviceIdType.MESH)

    @pl.when(has_up)
    def _():
        pl.semaphore_signal(barrier, inc=1, device_id=up_dev, device_id_type=pl.DeviceIdType.MESH)

    @pl.when(has_down)
    def _():
        pl.semaphore_signal(barrier, inc=1, device_id=down_dev, device_id_type=pl.DeviceIdType.MESH)

    small = [
        pltpu.make_async_copy(incl_hbm, incl, in_sem.at[0]),
        pltpu.make_async_copy(mean_hbm, mean, in_sem.at[1]),
    ]
    sets = chunks // per
    ahead = 1
    loop(ahead, load_group)
    pl.semaphore_wait(barrier, 2 + has_up.astype(jnp.int32) + has_down.astype(jnp.int32))

    for copy in small:
        copy.start()

    eta[...] = jnp.zeros_like(eta)
    scale = scale_ref[...]
    shrink = scale / (1.0 + scale)
    bias = prior_ref[...] - 0.5 * jnp.log1p(scale)
    curve = 0.5 * total * shrink

    def among(s, which):
        found = s < 0
        for k in which:
            found = found | (s == k)
        return found

    def reduce_wide(s):
        return among(s, REDUCE_WIDE)

    def gather_wide(s):
        return among(s, GATHER_WIDE)

    def product(g, yy, cc, out):
        for_z(lambda i: load(g, i, yy, cc).wait())

        def piece(j):
            out[wide_span(4 * j, 4), :] = lax.dot_general(
                geno[g, :, wide_span(place_of(4 * j, yy, cc), 4)], resid_ref[...], (((0,), (0,)), ((), ())),
                preferred_element_type=jnp.float32,
            )

        loop(length // 4, piece)

    def core_copy(g, h):
        return remote(
            core_out.at[lax.rem(g, slots), h], core_in.at[g, h], core_ss.at[g, h], core_rs.at[g, h], core_dev
        )

    def pair_copy(s, j):
        return remote(
            pair_out.at[s, nth(j)], pair_in.at[s, nth(j)], pair_ss.at[s], pair_rs.at[s, j], pair_dev
        )

    def pair_all(s):
        return remote(pair_out.at[s], pair_in.at[s], pair_ss.at[s], pair_rs.at[s, 0], pair_dev)

    def line_copy(s, t, d, f):
        return remote(
            line_out.at[s, t, d, f], line_in.at[s, t, d, f], line_ss.at[s, t, d, f], line_rs.at[s, t, d, f],
            up_dev if d == 0 else down_dev,
        )

    def to_core(g, h, yy):
        @pl.when(g >= slots)
        def _():
            core_copy(g - slots, h).wait_send()

        product(g, yy, 1 - c, core_out.at[lax.rem(g, slots), h])
        core_copy(g, h).start()

    def first_core(g):
        to_core(g, 0, 1 - y)

        @pl.when(g + ahead < sets)
        def _():
            load_group(g + ahead)

    def first_own(g):
        product(g, 1 - y, c, own.at[g, 1])

    def first_pair(g):
        core_copy(g, 0).wait_recv()

        def one(k):
            s = g * per + k

            @pl.when(jnp.logical_not(reduce_wide(s)))
            def _():
                def piece(j):
                    part = span(s, far(j))
                    pair_out[s, nth(j)] = encode(own[g, 1, part] + core_in[g, 0, part])
                    pair_copy(s, j).start()

                for_z(piece)

            @pl.when(reduce_wide(s))
            def _():
                def piece(j):
                    part = span(s, j)
                    own[g, 1, part] = own[g, 1, part] + core_in[g, 0, part]

                for_z(piece)

        loop(per, one)

    def second_core(g):
        to_core(g, 1, y)
        product(g, y, c, own.at[g, 0])

    def second_own(g):
        @pl.when(g == 0)
        def _():
            for copy in small:
                copy.wait()

        core_copy(g, 1).wait_recv()

        def piece(j):
            part = wide_span(4 * j, 4)
            own[g, 0, part] = own[g, 0, part] + core_in[g, 1, part]

        loop(length // 4, piece)

    def from_pair(s, j):
        part = span(s, far(j))
        pair_copy(s, j).wait_recv()
        own[s // per, 0, part] = own[s // per, 0, part] + decode(pair_in[s, nth(j)])

    def line_ends(s, t, wide):
        for d in range(2):
            place = z if d == 0 else length - 1 - z
            block = length - 1 - t if d == 0 else t

            @pl.when(place == 0)
            def _():
                for f in range(2 if wide else 1):
                    line_out[s, t, d, f] = encode(own[s // per, f, span(s, block)])
                    line_copy(s, t, d, f).start()

    def along(s, t, wide):
        for d in range(2):
            place = z if d == 0 else length - 1 - z
            block = length - 1 - t + z if d == 0 else t - (length - 1 - z)

            @pl.when((place > 0) & (place <= t) & (place < length - 1))
            def _():
                for f in range(2 if wide else 1):
                    line_copy(s, t - 1, d, f).wait_recv()
                    line_out[s, t, d, f] = encode(
                        own[s // per, f, span(s, block)] + decode(line_in[s, t - 1, d, f])
                    )
                    line_copy(s, t, d, f).start()

    def arrive(s, wide):
        mine = span(s, z)
        for f in range(2 if wide else 1):
            for d in range(2):
                @pl.when(has_down if d == 0 else has_up)
                def _():
                    line_copy(s, length - 2, d, f).wait_recv()
                    own[s // per, f, mine] = own[s // per, f, mine] + decode(line_in[s, length - 2, d, f])

        if wide:
            pair_out[s, nth(0)] = encode(own[s // per, 1, mine])
            pair_copy(s, 0).start()

    def gz_copy(s, u, d, f):
        k, q = 2 * s + f, span(s, place_of(z - u if d == 0 else z + u, y if f == 0 else 1 - y, c))
        return remote(
            eff.at[s // per, q], eff.at[s // per, q], gz_ss.at[k, u, d], gz_rs.at[k, u, d], up_dev if d == 0 else down_dev
        )

    def gz_landed(s, u, d, f):
        k, q = 2 * s + f, span(s, place_of(z - 1 - u if d == 0 else z + 1 + u, y if f == 0 else 1 - y, c))
        return remote(
            eff.at[s // per, q], eff.at[s // per, q], gz_ss.at[k, u, d], gz_rs.at[k, u, d], up_dev if d == 0 else down_dev
        )

    def gy_copy(s, i, yy):
        q = span(s, place_of(i, yy, c))
        return remote(eff.at[s // per, q], eff.at[s // per, q], gy_ss.at[s], gy_rs.at[s, i], pair_dev)

    def gc_copy(s, i, yy, cc):
        q = span(s, place_of(i, yy, cc))
        return remote(eff.at[s // per, q], eff.at[s // per, q], gc_ss.at[s], gc_rs.at[s], core_dev)

    def gy_sent(s, count):
        q = wide_span(0, count)
        return remote(eff.at[s, q], eff.at[s, q], gy_ss.at[s], gy_rs.at[s, 0], pair_dev)

    def gc_all(s, first, count):
        q = wide_span(first, count)
        return remote(eff.at[s, q], eff.at[s, q], gc_ss.at[s], gc_rs.at[s], core_dev)

    def use(g, cc):
        def piece(j):
            q = wide_span(place_of(0, 0, cc) + 8 * j, 8)
            eta[...] += jnp.dot(geno[g, :, q], eff[g, q], preferred_element_type=jnp.float32)

        loop(length // 4, piece)

    def send_own(s, f):
        @pl.when(has_up)
        def _():
            gz_copy(s, 0, 0, f).start()

        @pl.when(has_down)
        def _():
            gz_copy(s, 0, 1, f).start()

        gc_copy(s, z, y if f == 0 else 1 - y, c).start()

    def finish(s, wide):
        g, mine = s // per, span(s, z)
        if wide:
            pair_copy(s, 0).wait_recv()
            own[g, 0, mine] = own[g, 0, mine] + decode(pair_in[s, nth(0)])
        here = pl.ds(pl.multiple_of(s * rows, 8), rows)
        before = incl[here, :]
        stat = own[g, 0, mine] / total + before * mean[here, :]
        stat_out[here, :] = stat
        incl_new = 0.5 * before + 0.5 * jax.nn.sigmoid(bias + curve * stat * stat)
        eff[g, span(s, place_of(z, y, c))] = (incl_new * (stat * shrink)).astype(jnp.bfloat16)
        gy_copy(s, z, y).start()
        send_own(s, 0)

    def send_other(s):
        gy_copy(s, z, 1 - y).wait_recv()

        @pl.when(even)
        def _():
            gz_copy(s, 0, 0, 1).start()

        @pl.when(jnp.logical_not(even))
        def _():
            gz_copy(s, 0, 1, 1).start()

        gc_copy(s, z, 1 - y, c).start()

    def take_other(s):
        @pl.when(even)
        def _():
            gz_landed(s, 0, 1, 1).wait_recv()

        @pl.when(jnp.logical_not(even))
        def _():
            gz_landed(s, 0, 0, 1).wait_recv()

        gc_copy(s, mate, 1 - y, c).start()

    def spread(s, u, f, wide):
        for d in range(2):
            source = z - u if d == 0 else z + u

            @pl.when((source >= 0) & (source < length))
            def _():
                gz_landed(s, u - 1, d, f).wait_recv()

                if u < length - 1:
                    @pl.when(has_up if d == 0 else has_down)
                    def _():
                        gz_copy(s, u, d, f).start()

                if wide and u == 1:
                    @pl.when(source != mate)
                    def _():
                        gy_copy(s, source, y).start()
                else:
                    gy_copy(s, source, y).start()

                gc_copy(s, source, y if f == 0 else 1 - y, c).start()

    def last_pair(s):
        for_z(lambda i: gy_copy(s, i, 1 - y).wait_recv())
        gc_all(s, place_of(0, 1 - y, c), length).start()

    def last_others(s):
        def take(i):
            @pl.when((i != z) & (i != mate))
            def _():
                gy_copy(s, i, 1 - y).wait_recv()
                gc_copy(s, i, 1 - y, c).start()

        for_z(take)

    def drain(s):
        @pl.when((s % per == 0) & (s // per >= chunks // per - slots))
        def _():
            for h in range(2):
                core_copy(s // per, h).wait_send()

        @pl.when(reduce_wide(s))
        def _():
            pair_copy(s, 0).wait_send()

        @pl.when(jnp.logical_not(reduce_wide(s)))
        def _():
            pair_all(s).wait_send()

        @pl.when(gather_wide(s))
        def _():
            gy_sent(s, length - 1).wait_send()

            @pl.when(even)
            def _():
                gz_copy(s, 0, 0, 1).wait_send()

            @pl.when(jnp.logical_not(even))
            def _():
                gz_copy(s, 0, 1, 1).wait_send()

        @pl.when(jnp.logical_not(gather_wide(s)))
        def _():
            gy_sent(s, length).wait_send()

        gc_all(s, place_of(0, 0, c), 2 * length).wait_send()

        def step(t):
            for d in range(2):
                place = z if d == 0 else length - 1 - z
                origin = z - t if d == 0 else z + t

                @pl.when((place <= t) & (place < length - 1))
                def _():
                    line_copy(s, t, d, 0).wait_send()

                    @pl.when(reduce_wide(s))
                    def _():
                        line_copy(s, t, d, 1).wait_send()

                @pl.when((origin >= 0) & (origin < length) & (place < length - 1))
                def _():
                    gz_copy(s, t, d, 0).wait_send()

        loop(length - 1, step)

    def use_own(g):
        use(g, c)

    def use_core(g):
        gc_all(g, place_of(0, 0, 1 - c), 2 * length).wait_recv()
        use(g, 1 - c)
        drain(g)

    groups = {
        "P0": first_core, "P1": first_own, "P2": first_pair, "P3": second_core, "P4": second_own,
        "U1": use_own, "U2": use_core,
    }
    tasks = {
        "OT": (gather_wide, True, send_other), "h1Z": (gather_wide, True, take_other),
        "LA": (gather_wide, False, last_pair), "LAZ": (gather_wide, True, last_others),
    }
    for j in range(length):
        tasks[f"D{j}Y"] = (reduce_wide, False, functools.partial(from_pair, j=j))
    for kind in "YZ":
        wide = kind == "Z"
        for t in range(length - 1):
            tasks[f"E{t}{kind}"] = (reduce_wide, wide, functools.partial(line_ends, t=t, wide=wide))
            if t > 0:
                tasks[f"T{t}{kind}"] = (reduce_wide, wide, functools.partial(along, t=t, wide=wide))
        tasks["AR" + kind] = (reduce_wide, wide, functools.partial(arrive, wide=wide))
        tasks["FI" + kind] = (reduce_wide, wide, functools.partial(finish, wide=wide))
        for u in range(1, length):
            tasks[f"g{u}{kind}"] = (gather_wide, wide, functools.partial(spread, u=u, f=0, wide=wide))

    steps = plan(length)
    names = [*groups, *tasks]
    least = min(math.floor(steps[name]) for name in names)
    late = {name: math.floor(steps[name]) - least for name in names}
    order = sorted(names, key=lambda name: steps[name] - math.floor(steps[name]))

    def wave(w):
        for name in order:
            s = w - late[name]
            go = (s >= 0) & (s < chunks)
            if name in groups:
                @pl.when(go & (s % per == 0))
                def _():
                    groups[name](s // per)
            else:
                test, wanted, body = tasks[name]

                @pl.when(go & (test(s) if wanted else jnp.logical_not(test(s))))
                def _():
                    body(s)

    loop(chunks + max(late.values()), wave)


def outputs_kernel(
    half_total, stat_ref, incl_ref, eta_ref, labels_ref, prior_ref, scale_ref, offset_ref,
    incl_out, mean_out, resid_out,
):
    scale = scale_ref[...]
    shrink = scale / (1.0 + scale)
    bias = prior_ref[...] - 0.5 * jnp.log1p(scale)
    stat = stat_ref[...]
    mean_out[...] = stat * shrink
    logit = bias + (half_total * shrink) * stat * stat
    incl_out[...] = 0.5 * incl_ref[...] + 0.5 * jax.nn.sigmoid(logit)
    resid_out[...] = 4.0 * (
        labels_ref[...].astype(jnp.float32) - jax.nn.sigmoid(eta_ref[...] + offset_ref[...])
    )


def on_device(genotype, residual, labels, incl_old, mean_old, prior_logit, slab_scale, offset):
    n = lax.axis_size("ind")
    people, _ = genotype.shape
    owned, columns = incl_old.shape
    length = n // 4
    per = 1
    chunks = per * max(1, min(8, owned // 128))
    sets = chunks // per
    slots = max(1, min(sets // 2, 3))
    rows = owned // chunks
    f32, bf16, i16 = jnp.float32, jnp.bfloat16, jnp.int16
    anywhere = pl.BlockSpec(memory_space=pl.ANY)
    vmem = pl.BlockSpec(memory_space=pltpu.VMEM)
    dma = pltpu.SemaphoreType.DMA
    hops = length - 1
    prior, scale, shift = (v.reshape(1, -1) for v in (prior_logit, slab_scale, offset))
    stat, eta = pl.pallas_call(
        functools.partial(sweep_kernel, n, chunks, per, slots),
        out_shape=(
            jax.ShapeDtypeStruct((owned, columns), f32),
            jax.ShapeDtypeStruct((people, columns), f32),
        ),
        in_specs=[anywhere, vmem, anywhere, anywhere, vmem, vmem],
        out_specs=(vmem, vmem),
        scratch_shapes=[
            pltpu.VMEM((sets, people, n * per * rows), bf16),
            pltpu.VMEM(incl_old.shape, f32),
            pltpu.VMEM(mean_old.shape, f32),
            pltpu.VMEM((slots, 2, length * per * rows, columns), f32),
            pltpu.VMEM((sets, 2, length * per * rows, columns), f32),
            pltpu.VMEM((chunks, length * rows, columns), i16),
            pltpu.VMEM((chunks, length * rows, columns), i16),
            pltpu.VMEM((sets, 2, length * per * rows, columns), f32),
            pltpu.VMEM((chunks, hops, 2, 2, rows, columns), i16),
            pltpu.VMEM((chunks, hops, 2, 2, rows, columns), i16),
            pltpu.VMEM((sets, n * per * rows, columns), bf16),
            dma((sets, n)),
            dma((2,)),
            dma((sets, 2)),
            dma((sets, 2)),
            dma((chunks,)),
            dma((chunks, length)),
            dma((chunks, hops, 2, 2)),
            dma((chunks, hops, 2, 2)),
            dma((2 * chunks, hops, 2)),
            dma((2 * chunks, hops, 2)),
            dma((chunks,)),
            dma((chunks, length)),
            dma((chunks,)),
            dma((chunks,)),
        ],
        compiler_params=pltpu.CompilerParams(
            collective_id=0, has_side_effects=True, vmem_limit_bytes=67043328
        ),
        name="sweep",
    )(genotype, residual, incl_old, mean_old, prior, scale)

    steps = 2 if owned % 32 == 0 and people % 32 == 0 else 1
    upper = pl.BlockSpec((owned // steps, columns), lambda i: (i, 0))
    lower = pl.BlockSpec((people // steps, columns), lambda i: (i, 0))
    flat = pl.BlockSpec((1, columns), lambda i: (0, 0))
    return pl.pallas_call(
        functools.partial(outputs_kernel, 0.5 * people * n),
        grid=(steps,),
        out_shape=(
            jax.ShapeDtypeStruct((owned, columns), f32),
            jax.ShapeDtypeStruct((owned, columns), f32),
            jax.ShapeDtypeStruct((people, columns), f32),
        ),
        in_specs=[upper, upper, lower, lower, flat, flat, flat],
        out_specs=(upper, upper, lower),
        name="outputs",
    )(stat, incl_old, eta, labels, prior, scale, shift)


def solution(mesh):
    placed = (
        P(("groups", "ind"), None),
        P(("groups", "ind"), None),
        P(("groups", "ind"), None),
        P(("groups", "ind"), None),
        P(("groups", "ind"), None),
        P(),
        P(),
        P(),
    )
    return jax.shard_map(
        on_device,
        mesh=mesh,
        in_specs=placed,
        out_specs=(
            P(("groups", "ind"), None),
            P(("groups", "ind"), None),
            P(("groups", "ind"), None),
        ),
        check_vma=False,
    )
```
